32 devices in a mesh: group: 2 (over x), rows: 16 (over z, y, core).
Axes of the slice: x: 2, y: 2, z: 4, core: 2. Of those that a mesh axis runs over, the one named last changes fastest.
Arguments:
- queries: bfloat16 [256, 3072], P(('group', 'rows')), parts along dimension 0, may hold values from -200 to 200
- prefix_keys: bfloat16 [2048, 1024], P(('group', 'rows')), parts along dimension 0, may hold values from -6 to 6
- prefix_values: bfloat16 [2048, 1024], P(('group', 'rows')), parts along dimension 0, may hold values from -6 to 6
- tree_keys: bfloat16 [256, 1024], P(('group', 'rows')), parts along dimension 0, may hold values from -12 to 12
- tree_values: bfloat16 [256, 1024], P(('group', 'rows')), parts along dimension 0, may hold values from -6 to 6
- parents: int32 [256], P('group'), parts along dimension 0, may hold values from 0 to 95, as said below
Outputs:
- attended: bfloat16 [256, 3072], P(('group', 'rows')), parts along dimension 0
The draws below stay inside these ranges and needn't reach their ends.
There are 2 independent parts, one for each index of `group`. The reference program is written for one: setup_inputs(seed, part) draws one part's arguments, and reference() takes and returns one part's arrays. A program takes and returns all parts, laid end to end along the dimension named above; each array names one. Nothing has to cross between parts.
Inputs may be any that keep to these rules, and one draw needn't show every extreme that they name: `parents`: the rows hold the candidate trees of many requests, in 4 levels of 32 rows in order; a row of the first level is a tree's root and its own parent; every other row's parent is a row of the level before its own, and the first and the last row of each later level have the last row of the level before as parent.
All inputs are finite; a program needn't handle non-finite values.
Results may differ from the reference program's by a relative error of at most 0.005.
Values may be sent and summed in bfloat16 or wider, within the bound.
A program may use at most 192 MiB of HBM per device.

```python
import jax
import jax.numpy as jnp
from jax import lax

QUERY_HEADS = 24
KV_HEADS = 8
HEAD_DIM = 128
TREE_DEPTH = 4
PREFIX = 1024
CANDIDATES = 128
LEVEL_ROWS = 32


def common_terms(key):
    base = jax.random.fold_in(key, 4242)
    first, second, third = jax.random.split(base, 3)
    direction = jax.random.normal(first, (KV_HEADS, HEAD_DIM), jnp.float32)
    direction = direction * jnp.sqrt(HEAD_DIM / jnp.sum(direction * direction, axis=1, keepdims=True))
    floor_level = jnp.log(jnp.float32(PREFIX))
    boost = floor_level + jax.random.uniform(second, (CANDIDATES,), jnp.float32, -2.5, 0.5)
    lift = 1.0 + 0.003 * jax.random.uniform(third, (CANDIDATES,), jnp.float32)
    return (direction, boost, lift)


def draw_queries(key, part):
    direction, boost, lift = common_terms(key)
    noise = jax.random.normal(jax.random.fold_in(key, 17), (CANDIDATES, KV_HEADS, QUERY_HEADS // KV_HEADS, HEAD_DIM), jnp.float32)
    along = (boost / jnp.sqrt(jnp.float32(HEAD_DIM)))[:, None, None, None] * direction[None, :, None, :]
    summed = jnp.clip(noise + along, -200.0, 200.0)
    return summed.reshape(CANDIDATES, QUERY_HEADS * HEAD_DIM).astype(jnp.bfloat16)


def draw_tree_keys(key, part):
    direction, boost, lift = common_terms(key)
    noise = jax.random.normal(jax.random.fold_in(key, 29), (CANDIDATES, KV_HEADS, HEAD_DIM), jnp.float32)
    inner = jnp.sum(noise * direction[None], axis=2, keepdims=True) / HEAD_DIM
    keyed = noise - inner * direction[None] + lift[:, None, None] * direction[None]
    keyed = jnp.clip(keyed, -12.0, 12.0)
    return keyed.reshape(CANDIDATES, KV_HEADS * HEAD_DIM).astype(jnp.bfloat16)


def draw_parents(key, part):
    row_ids = jnp.arange(CANDIDATES, dtype=jnp.int32)
    tier = row_ids // LEVEL_ROWS
    lowest = jnp.maximum(tier - 1, 0) * LEVEL_ROWS
    picks = jax.random.randint(jax.random.fold_in(key, 11), (CANDIDATES,), 0, LEVEL_ROWS, dtype=jnp.int32)
    chosen = lowest + picks
    within = row_ids % LEVEL_ROWS
    closing = (within == LEVEL_ROWS - 1) | (within == 0)
    chosen = jnp.where(closing, lowest + LEVEL_ROWS - 1, chosen)
    return jnp.where(tier == 0, row_ids, chosen).astype(jnp.int32)


def level_of(own_key, dims, pieces, smallest, high):
    def one(axis_at, shards_of):
        steps = jax.random.uniform(jax.random.fold_in(jax.random.fold_in(own_key, 6), axis_at), (shards_of,), jnp.float32, smallest / len(pieces), high / len(pieces))
        return jnp.repeat(jnp.exp(steps), dims[axis_at] // shards_of).reshape((-1,) + (1,) * (len(dims) - axis_at - 1))

    factor_of = one(*pieces[0])
    for cut in pieces[1:]:
        factor_of = factor_of * one(*cut)
    return factor_of


def bell_draw(own_key, extent, spread, limit, cuts=(), kind=jnp.bfloat16):
    entries = jax.random.normal(own_key, extent, jnp.float32) * spread
    if len(cuts) > 0:
        entries = level_of(own_key, extent, cuts, -0.22, 0.18) * entries
    return jnp.clip(entries, min=-limit, max=limit).astype(kind)


def setup_inputs(seed: int = 0, part: int = 0) -> dict:
    arg_keys = jax.random.split(jax.random.key(seed), 7)
    part_keys = jax.random.split(jax.random.fold_in(arg_keys[6], part), 7)
    queries = draw_queries(jax.random.fold_in(jax.random.fold_in(arg_keys[6], part), 71), part)
    prefix_keys = bell_draw(part_keys[1], (PREFIX, KV_HEADS * HEAD_DIM), 1.0, 6.0, ((0, 16),))
    prefix_values = bell_draw(part_keys[2], (PREFIX, KV_HEADS * HEAD_DIM), 1.0, 6.0, ((0, 16),))
    tree_keys = draw_tree_keys(jax.random.fold_in(jax.random.fold_in(arg_keys[6], part), 71), part)
    tree_values = bell_draw(part_keys[4], (CANDIDATES, KV_HEADS * HEAD_DIM), 1.0, 6.0, ((0, 16),))
    parents = draw_parents(jax.random.fold_in(jax.random.fold_in(arg_keys[6], part), 71), part)
    return dict(queries=queries, prefix_keys=prefix_keys, prefix_values=prefix_values, tree_keys=tree_keys, tree_values=tree_values, parents=parents)


def lineage_mask(parents, row_ids):
    walker = row_ids
    columns = jnp.arange(parents.shape[0], dtype=jnp.int32)
    allowed = walker[:, None] == columns[None, :]
    for level_step in range(TREE_DEPTH - 1):
        walker = parents[walker]
        allowed = allowed | (walker[:, None] == columns[None, :])
    return allowed


def reference(queries, prefix_keys, prefix_values, tree_keys, tree_values, parents):
    groups = QUERY_HEADS // KV_HEADS
    block = 16
    every_key = jnp.concatenate([prefix_keys, tree_keys], axis=0).astype(jnp.float32).reshape(-1, KV_HEADS, HEAD_DIM)
    every_value = jnp.concatenate([prefix_values, tree_values], axis=0).astype(jnp.float32).reshape(-1, KV_HEADS, HEAD_DIM)
    blocks = queries.reshape(CANDIDATES // block, block, KV_HEADS, groups, HEAD_DIM)
    starts = jnp.arange(CANDIDATES // block, dtype=jnp.int32) * block

    def attend(inputs):
        query_block, first_row = inputs
        row_ids = first_row + jnp.arange(block, dtype=jnp.int32)
        allowed = lineage_mask(parents, row_ids)
        visible = jnp.concatenate([jnp.ones((block, PREFIX), jnp.int32) == 1, allowed], axis=1)
        scores = jnp.einsum("rkgd,skd->rkgs", query_block.astype(jnp.float32), every_key) * HEAD_DIM ** -0.5
        scores = jnp.where(visible[:, None, None, :], scores, -jnp.inf)
        maxima = jnp.max(scores, axis=-1, keepdims=True)
        weights = jnp.exp(scores - maxima)
        masses = jnp.sum(weights, axis=-1)
        rounded = lax.optimization_barrier(weights.astype(jnp.bfloat16)).astype(jnp.float32)
        weighted = jnp.einsum("rkgs,skd->rkgd", rounded, every_value)
        result = weighted / masses[..., None]
        return result.reshape(block, QUERY_HEADS * HEAD_DIM).astype(jnp.bfloat16)

    return lax.map(attend, (blocks, starts)).reshape(CANDIDATES, QUERY_HEADS * HEAD_DIM)
```

```python
import functools

import jax
import jax.numpy as jnp
from jax import lax
from jax.experimental import pallas as pl
from jax.experimental.pallas import tpu as pltpu
from jax.sharding import PartitionSpec as P

QUERY_HEADS = 24
KV_HEADS = 8
HEAD_DIM = 128
TREE_DEPTH = 4
GROUPS = QUERY_HEADS // KV_HEADS
WIDTH = GROUPS * HEAD_DIM
PART = 32

LAST = (((1,), (1,)), ((), ()))
MESH = pl.DeviceIdType.MESH


def pack_stats(maxima, masses):
    rows = maxima[0].shape[0]
    lane = lax.broadcasted_iota(jnp.int32, (rows, HEAD_DIM), 1)
    place = lane % PART
    stat = jnp.zeros((rows, HEAD_DIM), jnp.float32)
    for at, column in enumerate(maxima + masses):
        stat = jnp.where(place == at, column, stat)
    high = stat.astype(jnp.bfloat16).astype(jnp.float32)
    rest = stat - high
    middle = rest.astype(jnp.bfloat16).astype(jnp.float32)
    low = rest - middle
    return jnp.where(lane < PART, high, jnp.where(lane < 2 * PART, middle, low))


def kernel(
    n, q_in, pk_in, pv_in, tk_in, tv_in, parents, out,
    qbuf, kbuf, vbuf, tbuf, obuf, rbuf, mask,
    sem_q, sem_k, sem_v, sem_t, sem_r, send_q, send_k, send_v, send_t, send_r,
):
    me = lax.axis_index("rows")
    local = q_in.shape[0]
    blocks = n // KV_HEADS
    block_rows = KV_HEADS * local
    my_block = me // KV_HEADS
    my_slot = me % KV_HEADS

    def send(src, dst, send_sem, recv_sem, to):
        pltpu.make_async_remote_copy(
            src_ref=src, dst_ref=dst, send_sem=send_sem, recv_sem=recv_sem,
            device_id={"rows": to}, device_id_type=MESH,
        ).start()

    def settle(ref, sem):
        pltpu.make_async_copy(ref, ref, sem).wait()

    def columns(ref, head, width):
        return ref.at[:, pl.ds(pl.multiple_of(head * width, width), width)]

    barrier = pltpu.get_barrier_semaphore()
    for step in range(1, n):
        pl.semaphore_signal(
            barrier, inc=1, device_id={"rows": (me + step) % n}, device_id_type=MESH
        )
    pltpu.make_async_copy(columns(q_in, my_slot, WIDTH), qbuf.at[me], sem_q.at[my_block]).start()
    pltpu.make_async_copy(columns(pk_in, my_slot, HEAD_DIM), kbuf.at[my_slot], sem_k).start()
    pltpu.make_async_copy(columns(tk_in, my_slot, HEAD_DIM), tbuf.at[0, my_slot], sem_t).start()
    pltpu.make_async_copy(columns(tv_in, my_slot, HEAD_DIM), tbuf.at[1, my_slot], sem_t).start()
    pltpu.make_async_copy(columns(pv_in, my_slot, HEAD_DIM), vbuf.at[my_slot], sem_v).start()
    pl.semaphore_wait(barrier, n - 1)

    for far in range(1, blocks):
        for step in range(KV_HEADS):
            head = (my_slot + step) % KV_HEADS
            to = (my_block + far) % blocks * KV_HEADS + head
            send(columns(q_in, head, WIDTH), qbuf.at[me], send_q, sem_q.at[my_block], to)
    for step in range(1, KV_HEADS):
        head = (my_slot + step) % KV_HEADS
        to = my_block * KV_HEADS + head
        send(columns(q_in, head, WIDTH), qbuf.at[me], send_q, sem_q.at[my_block], to)
        send(columns(tk_in, head, HEAD_DIM), tbuf.at[0, my_slot], send_t, sem_t, to)
        send(columns(pk_in, head, HEAD_DIM), kbuf.at[my_slot], send_k, sem_k, to)
    for step in range(1, KV_HEADS):
        head = (my_slot + step) % KV_HEADS
        to = my_block * KV_HEADS + head
        send(columns(tv_in, head, HEAD_DIM), tbuf.at[1, my_slot], send_t, sem_t, to)
        send(columns(pv_in, head, HEAD_DIM), vbuf.at[my_slot], send_v, sem_v, to)

    count = parents.shape[1]
    parent = jnp.broadcast_to(parents[...], (count, count))
    token = lax.broadcasted_iota(jnp.int32, (count, count), 0)
    row = lax.broadcasted_iota(jnp.int32, (count, count), 1)
    hop = (parent == token).astype(jnp.float32).astype(jnp.bfloat16)
    mine = lax.broadcasted_iota(jnp.int32, (block_rows, count), 0) + my_block * block_rows
    own = lax.broadcasted_iota(jnp.int32, (block_rows, count), 1)
    member = (mine == own).astype(jnp.float32)
    seen = member
    for _ in range(TREE_DEPTH - 1):
        member = jnp.dot(member.astype(jnp.bfloat16), hop, preferred_element_type=jnp.float32)
        seen = seen + member
    same = (token == row).astype(jnp.float32).astype(jnp.bfloat16)
    mask[...] = lax.dot_general(
        same, seen.astype(jnp.bfloat16), LAST, preferred_element_type=jnp.float32
    )

    for order in range(blocks):
        block = (my_block + 1 + order) % blocks
        first = pl.multiple_of(block * KV_HEADS, KV_HEADS)
        settle(qbuf.at[pl.ds(0, KV_HEADS)], sem_q.at[block])
        if order == 0:
            settle(kbuf, sem_k)
            settle(tbuf, sem_t)
            settle(vbuf, sem_v)
        keys = kbuf[...].reshape(-1, HEAD_DIM)
        tree_keys = tbuf[0].astype(jnp.float32).reshape(block_rows, HEAD_DIM).astype(jnp.bfloat16)
        values = vbuf[...].reshape(-1, HEAD_DIM)
        tree_values = tbuf[1].astype(jnp.float32).reshape(block_rows, HEAD_DIM).astype(jnp.bfloat16)
        queries = qbuf[pl.ds(first, KV_HEADS)].astype(jnp.float32).reshape(block_rows, WIDTH)
        visible = mask[pl.ds(pl.multiple_of(block * block_rows, block_rows), block_rows), :] > 0.5
        pieces, maxima, masses = [], [], []
        for group in range(GROUPS):
            query = queries[:, group * HEAD_DIM : (group + 1) * HEAD_DIM].astype(jnp.bfloat16)
            scale = HEAD_DIM ** (-0.5)
            slab = lax.dot_general(query, keys, LAST, preferred_element_type=jnp.float32) * scale
            tree = (
                lax.dot_general(query, tree_keys, LAST, preferred_element_type=jnp.float32) * scale
            )
            tree = jnp.where(visible, tree, -jnp.inf)
            top = jnp.maximum(
                jnp.max(slab, axis=1, keepdims=True), jnp.max(tree, axis=1, keepdims=True)
            )
            slab = jnp.exp(slab - top)
            tree = jnp.exp(tree - top)
            maxima.append(top)
            masses.append(
                jnp.sum(slab, axis=1, keepdims=True) + jnp.sum(tree, axis=1, keepdims=True)
            )
            pieces.append(
                jnp.dot(slab.astype(jnp.bfloat16), values, preferred_element_type=jnp.float32)
                + jnp.dot(
                    tree.astype(jnp.bfloat16), tree_values, preferred_element_type=jnp.float32
                )
            )
        pieces.append(pack_stats(maxima, masses))
        packed = jnp.concatenate(pieces, axis=1).reshape(KV_HEADS, local, WIDTH + HEAD_DIM)
        obuf[pl.ds(first, KV_HEADS)] = packed.astype(jnp.bfloat16)
        for step in range(KV_HEADS):
            if order == blocks - 1 and step == 0:
                pltpu.make_async_copy(obuf.at[me], rbuf.at[me], sem_r).start()
            else:
                to = first + (my_slot + step) % KV_HEADS
                send(obuf.at[to], rbuf.at[me], send_r, sem_r, to)

    settle(qbuf.at[pl.ds(0, n - 1)], send_q)
    settle(kbuf.at[pl.ds(0, KV_HEADS - 1)], send_k)
    settle(vbuf.at[pl.ds(0, KV_HEADS - 1)], send_v)
    settle(tbuf.at[:, pl.ds(0, KV_HEADS - 1)], send_t)
    settle(rbuf, sem_r)

    stat = rbuf[:, :, WIDTH:].astype(jnp.float32).reshape(n * local, HEAD_DIM)
    stat = (
        stat
        + pltpu.roll(stat, HEAD_DIM - PART, 1)
        + pltpu.roll(stat, HEAD_DIM - 2 * PART, 1)
    ).reshape(blocks, block_rows, HEAD_DIM)
    top = jnp.max(stat, axis=0)
    lane = lax.broadcasted_iota(jnp.int32, (block_rows, HEAD_DIM), 1)
    factors = []
    total = jnp.zeros((block_rows, HEAD_DIM), jnp.float32)
    for block in range(blocks):
        factor = jnp.exp(stat[block] - top)
        mass = pltpu.roll(stat[block], HEAD_DIM - GROUPS, 1)
        total = total + factor * mass
        factors.append(factor)
    total = jnp.where(lane < GROUPS, total, 1.0)
    factors = [factor / total for factor in factors]
    for head in range(KV_HEADS):
        for group in range(GROUPS):
            result = jnp.zeros((local, HEAD_DIM), jnp.float32)
            for block in range(blocks):
                share = factors[block][head * local : (head + 1) * local, group : group + 1]
                piece = rbuf[block * KV_HEADS + head, :, group * HEAD_DIM : (group + 1) * HEAD_DIM]
                result = result + piece.astype(jnp.float32) * share
            at = head * WIDTH + group * HEAD_DIM
            out[:, at : at + HEAD_DIM] = result.astype(out.dtype)
    settle(rbuf.at[pl.ds(0, n - 1)], send_r)


def shards(n, queries, prefix_keys, prefix_values, tree_keys, tree_values, parents):
    local = queries.shape[0]
    tokens = prefix_keys.shape[0]
    kind = queries.dtype
    blocks = n // KV_HEADS
    hbm = pl.BlockSpec(memory_space=pl.ANY)
    vmem = pl.BlockSpec(memory_space=pltpu.VMEM)
    dma = pltpu.SemaphoreType.DMA
    return pl.pallas_call(
        functools.partial(kernel, n),
        out_shape=jax.ShapeDtypeStruct(queries.shape, kind),
        in_specs=[hbm] * 5 + [vmem],
        out_specs=vmem,
        scratch_shapes=[
            pltpu.VMEM((n, local, WIDTH), kind),
            pltpu.VMEM((KV_HEADS, tokens, HEAD_DIM), kind),
            pltpu.VMEM((KV_HEADS, tokens, HEAD_DIM), kind),
            pltpu.VMEM((2, KV_HEADS, local, HEAD_DIM), kind),
            pltpu.VMEM((n, local, WIDTH + HEAD_DIM), kind),
            pltpu.VMEM((n, local, WIDTH + HEAD_DIM), kind),
            pltpu.VMEM((n * local, KV_HEADS * local), jnp.float32),
            dma((blocks,)), dma, dma, dma, dma, dma, dma, dma, dma, dma,
        ],
        compiler_params=pltpu.CompilerParams(collective_id=0, has_side_effects=True),
        name="tree_attention",
    )(queries, prefix_keys, prefix_values, tree_keys, tree_values, parents.reshape(1, -1))


def solution(mesh):
    placed = (
        P(("group", "rows"), None),
        P(("group", "rows"), None),
        P(("group", "rows"), None),
        P(("group", "rows"), None),
        P(("group", "rows"), None),
        P("group"),
    )
    return jax.shard_map(
        functools.partial(shards, mesh.shape["rows"]),
        mesh=mesh,
        in_specs=placed,
        out_specs=P(("group", "rows"), None),
        check_vma=False,
    )
```

```python
import functools

import jax
import jax.numpy as jnp
from jax import lax
from jax.experimental import pallas as pl
from jax.experimental.pallas import tpu as pltpu
from jax.sharding import PartitionSpec as P

QUERY_HEADS = 24
KV_HEADS = 8
HEAD_DIM = 128
TREE_DEPTH = 4
GROUPS = QUERY_HEADS // KV_HEADS
WIDTH = GROUPS * HEAD_DIM
PART = 32

LAST = (((1,), (1,)), ((), ()))
MESH = pl.DeviceIdType.MESH


def pack_stats(maxima, masses):
    rows = maxima[0].shape[0]
    lane = lax.broadcasted_iota(jnp.int32, (rows, HEAD_DIM), 1)
    place = lane % PART
    stat = jnp.zeros((rows, HEAD_DIM), jnp.float32)
    for at, column in enumerate(maxima + masses):
        stat = jnp.where(place == at, column, stat)
    high = stat.astype(jnp.bfloat16).astype(jnp.float32)
    rest = stat - high
    middle = rest.astype(jnp.bfloat16).astype(jnp.float32)
    low = rest - middle
    return jnp.where(lane < PART, high, jnp.where(lane < 2 * PART, middle, low))


def kernel(
    n, q_in, pk_in, pv_in, tk_in, tv_in, parents, out,
    qbuf, kbuf, vbuf, tbuf, obuf, rbuf, mask,
    sem_q, sem_k, sem_v, sem_t, sem_r, send_q, send_k, send_v, send_t, send_r,
):
    me = lax.axis_index("rows")
    local = q_in.shape[0]
    blocks = n // KV_HEADS
    block_rows = KV_HEADS * local
    my_block = me // KV_HEADS
    my_slot = me % KV_HEADS

    def send(src, dst, send_sem, recv_sem, to):
        pltpu.make_async_remote_copy(
            src_ref=src, dst_ref=dst, send_sem=send_sem, recv_sem=recv_sem,
            device_id={"rows": to}, device_id_type=MESH,
        ).start()

    def settle(ref, sem):
        pltpu.make_async_copy(ref, ref, sem).wait()

    def columns(ref, head, width):
        return ref.at[:, pl.ds(pl.multiple_of(head * width, width), width)]

    barrier = pltpu.get_barrier_semaphore()
    for step in range(1, n):
        pl.semaphore_signal(
            barrier, inc=1, device_id={"rows": (me + step) % n}, device_id_type=MESH
        )
    pltpu.make_async_copy(columns(q_in, my_slot, WIDTH), qbuf.at[me], sem_q.at[my_block]).start()
    pltpu.make_async_copy(columns(pk_in, my_slot, HEAD_DIM), kbuf.at[my_slot], sem_k).start()
    pltpu.make_async_copy(columns(tk_in, my_slot, HEAD_DIM), tbuf.at[0, my_slot], sem_t.at[0]).start()
    pltpu.make_async_copy(columns(tv_in, my_slot, HEAD_DIM), tbuf.at[1, my_slot], sem_t.at[1]).start()
    pltpu.make_async_copy(columns(pv_in, my_slot, HEAD_DIM), vbuf.at[my_slot], sem_v).start()
    pl.semaphore_wait(barrier, n - 1)

    for far in range(1, blocks):
        for step in range(KV_HEADS):
            head = (my_slot + step) % KV_HEADS
            to = (my_block + far) % blocks * KV_HEADS + head
            send(columns(q_in, head, WIDTH), qbuf.at[me], send_q, sem_q.at[my_block], to)
    for step in range(1, KV_HEADS):
        head = (my_slot + step) % KV_HEADS
        to = my_block * KV_HEADS + head
        send(columns(q_in, head, WIDTH), qbuf.at[me], send_q, sem_q.at[my_block], to)
        send(columns(tk_in, head, HEAD_DIM), tbuf.at[0, my_slot], send_t, sem_t.at[0], to)
        send(columns(pk_in, head, HEAD_DIM), kbuf.at[my_slot], send_k, sem_k, to)
    for step in range(1, KV_HEADS):
        head = (my_slot + step) % KV_HEADS
        to = my_block * KV_HEADS + head
        send(columns(tv_in, head, HEAD_DIM), tbuf.at[1, my_slot], send_t, sem_t.at[1], to)
        send(columns(pv_in, head, HEAD_DIM), vbuf.at[my_slot], send_v, sem_v, to)

    count = parents.shape[1]
    parent = jnp.broadcast_to(parents[...], (count, count))
    token = lax.broadcasted_iota(jnp.int32, (count, count), 0)
    row = lax.broadcasted_iota(jnp.int32, (count, count), 1)
    hop = (parent == token).astype(jnp.float32).astype(jnp.bfloat16)
    mine = lax.broadcasted_iota(jnp.int32, (block_rows, count), 0) + my_block * block_rows
    own = lax.broadcasted_iota(jnp.int32, (block_rows, count), 1)
    member = (mine == own).astype(jnp.float32)
    seen = member
    for _ in range(TREE_DEPTH - 1):
        member = jnp.dot(member.astype(jnp.bfloat16), hop, preferred_element_type=jnp.float32)
        seen = seen + member
    same = (token == row).astype(jnp.float32).astype(jnp.bfloat16)
    mask[...] = lax.dot_general(
        same, seen.astype(jnp.bfloat16), LAST, preferred_element_type=jnp.float32
    )

    settle(kbuf, sem_k)
    keys = kbuf[...].reshape(-1, HEAD_DIM)
    settle(tbuf.at[0], sem_t.at[0])
    tree_keys = tbuf[0].astype(jnp.float32).reshape(block_rows, HEAD_DIM).astype(jnp.bfloat16)
    scale = HEAD_DIM ** (-0.5)

    def weigh(block):
        first = pl.multiple_of(block * KV_HEADS, KV_HEADS)
        settle(qbuf.at[pl.ds(0, KV_HEADS)], sem_q.at[block])
        queries = qbuf[pl.ds(first, KV_HEADS)].astype(jnp.float32).reshape(block_rows, WIDTH)
        visible = mask[pl.ds(pl.multiple_of(block * block_rows, block_rows), block_rows), :] > 0.5
        weights, maxima, masses = [], [], []
        for group in range(GROUPS):
            query = queries[:, group * HEAD_DIM : (group + 1) * HEAD_DIM].astype(jnp.bfloat16)
            slab = lax.dot_general(query, keys, LAST, preferred_element_type=jnp.float32) * scale
            tree = (
                lax.dot_general(query, tree_keys, LAST, preferred_element_type=jnp.float32) * scale
            )
            tree = jnp.where(visible, tree, -jnp.inf)
            top = jnp.maximum(
                jnp.max(slab, axis=1, keepdims=True), jnp.max(tree, axis=1, keepdims=True)
            )
            slab = jnp.exp(slab - top)
            tree = jnp.exp(tree - top)
            maxima.append(top)
            masses.append(
                jnp.sum(slab, axis=1, keepdims=True) + jnp.sum(tree, axis=1, keepdims=True)
            )
            weights.append((slab.astype(jnp.bfloat16), tree.astype(jnp.bfloat16)))
        stats = pack_stats(maxima, masses).reshape(KV_HEADS, local, HEAD_DIM)
        obuf[pl.ds(first, KV_HEADS), :, WIDTH:] = stats.astype(jnp.bfloat16)
        return weights

    def values_ready():
        settle(vbuf, sem_v)
        settle(tbuf.at[1], sem_t.at[1])

    def apply(block, weights, last):
        first = pl.multiple_of(block * KV_HEADS, KV_HEADS)
        values = vbuf[...].reshape(-1, HEAD_DIM)
        tree_values = tbuf[1].astype(jnp.float32).reshape(block_rows, HEAD_DIM).astype(jnp.bfloat16)
        for group, (slab, tree) in enumerate(weights):
            piece = jnp.dot(slab, values, preferred_element_type=jnp.float32) + jnp.dot(
                tree, tree_values, preferred_element_type=jnp.float32
            )
            piece = piece.reshape(KV_HEADS, local, HEAD_DIM).astype(jnp.bfloat16)
            obuf[pl.ds(first, KV_HEADS), :, group * HEAD_DIM : (group + 1) * HEAD_DIM] = piece
        for step in range(KV_HEADS):
            if last and step == 0:
                pltpu.make_async_copy(obuf.at[me], rbuf.at[me], sem_r).start()
            else:
                to = first + (my_slot + step) % KV_HEADS
                send(obuf.at[to], rbuf.at[me], send_r, sem_r, to)

    order = [(my_block + 1 + step) % blocks for step in range(blocks)]
    ahead = [weigh(block) for block in order[:2]]
    values_ready()
    for step, block in enumerate(order):
        weights = ahead[step] if step < 2 else weigh(block)
        apply(block, weights, step == blocks - 1)

    settle(qbuf.at[pl.ds(0, n - 1)], send_q)
    settle(kbuf.at[pl.ds(0, KV_HEADS - 1)], send_k)
    settle(vbuf.at[pl.ds(0, KV_HEADS - 1)], send_v)
    settle(tbuf.at[:, pl.ds(0, KV_HEADS - 1)], send_t)
    settle(rbuf, sem_r)

    stat = rbuf[:, :, WIDTH:].astype(jnp.float32).reshape(n * local, HEAD_DIM)
    stat = (
        stat
        + pltpu.roll(stat, HEAD_DIM - PART, 1)
        + pltpu.roll(stat, HEAD_DIM - 2 * PART, 1)
    ).reshape(blocks, block_rows, HEAD_DIM)
    top = jnp.max(stat, axis=0)
    lane = lax.broadcasted_iota(jnp.int32, (block_rows, HEAD_DIM), 1)
    factors = []
    total = jnp.zeros((block_rows, HEAD_DIM), jnp.float32)
    for block in range(blocks):
        factor = jnp.exp(stat[block] - top)
        mass = pltpu.roll(stat[block], HEAD_DIM - GROUPS, 1)
        total = total + factor * mass
        factors.append(factor)
    total = jnp.where(lane < GROUPS, total, 1.0)
    factors = [factor / total for factor in factors]
    for head in range(KV_HEADS):
        for group in range(GROUPS):
            result = jnp.zeros((local, HEAD_DIM), jnp.float32)
            for block in range(blocks):
                share = factors[block][head * local : (head + 1) * local, group : group + 1]
                piece = rbuf[block * KV_HEADS + head, :, group * HEAD_DIM : (group + 1) * HEAD_DIM]
                result = result + piece.astype(jnp.float32) * share
            at = head * WIDTH + group * HEAD_DIM
            out[:, at : at + HEAD_DIM] = result.astype(out.dtype)
    settle(rbuf.at[pl.ds(0, n - 1)], send_r)


def shards(n, queries, prefix_keys, prefix_values, tree_keys, tree_values, parents):
    local = queries.shape[0]
    tokens = prefix_keys.shape[0]
    kind = queries.dtype
    blocks = n // KV_HEADS
    hbm = pl.BlockSpec(memory_space=pl.ANY)
    vmem = pl.BlockSpec(memory_space=pltpu.VMEM)
    dma = pltpu.SemaphoreType.DMA
    return pl.pallas_call(
        functools.partial(kernel, n),
        out_shape=pltpu.VMEM(queries.shape, kind),
        in_specs=[hbm] * 5 + [vmem],
        out_specs=vmem,
        scratch_shapes=[
            pltpu.VMEM((n, local, WIDTH), kind),
            pltpu.VMEM((KV_HEADS, tokens, HEAD_DIM), kind),
            pltpu.VMEM((KV_HEADS, tokens, HEAD_DIM), kind),
            pltpu.VMEM((2, KV_HEADS, local, HEAD_DIM), kind),
            pltpu.VMEM((n, local, WIDTH + HEAD_DIM), kind),
            pltpu.VMEM((n, local, WIDTH + HEAD_DIM), kind),
            pltpu.VMEM((n * local, KV_HEADS * local), jnp.float32),
            dma((blocks,)), dma, dma, dma((2,)), dma, dma, dma, dma, dma, dma,
        ],
        compiler_params=pltpu.CompilerParams(collective_id=0, has_side_effects=True),
        name="tree_attention",
    )(queries, prefix_keys, prefix_values, tree_keys, tree_values, parents.reshape(1, -1))


def solution(mesh):
    placed = (
        P(("group", "rows"), None),
        P(("group", "rows"), None),
        P(("group", "rows"), None),
        P(("group", "rows"), None),
        P(("group", "rows"), None),
        P("group"),
    )
    return jax.shard_map(
        functools.partial(shards, mesh.shape["rows"]),
        mesh=mesh,
        in_specs=placed,
        out_specs=P(("group", "rows"), None),
        check_vma=False,
    )
```

```python
import functools

import jax
import jax.numpy as jnp
from jax import lax
from jax.experimental import pallas as pl
from jax.experimental.pallas import tpu as pltpu
from jax.sharding import PartitionSpec as P

QUERY_HEADS = 24
KV_HEADS = 8
HEAD_DIM = 128
TREE_DEPTH = 4
GROUPS = QUERY_HEADS // KV_HEADS
WIDTH = GROUPS * HEAD_DIM
PART = 32

LAST = (((1,), (1,)), ((), ()))
MESH = pl.DeviceIdType.MESH


def pack_stats(maxima, masses):
    rows = maxima[0].shape[0]
    lane = lax.broadcasted_iota(jnp.int32, (rows, HEAD_DIM), 1)
    place = lane % PART
    stat = jnp.zeros((rows, HEAD_DIM), jnp.float32)
    for at, column in enumerate(maxima + masses):
        stat = jnp.where(place == at, column, stat)
    high = stat.astype(jnp.bfloat16).astype(jnp.float32)
    rest = stat - high
    middle = rest.astype(jnp.bfloat16).astype(jnp.float32)
    low = rest - middle
    return jnp.where(lane < PART, high, jnp.where(lane < 2 * PART, middle, low))


def kernel(
    n, q_in, pk_in, pv_in, tk_in, tv_in, parents_in, out,
    qbuf, kbuf, vbuf, tbuf, obuf, rbuf, mask, parents,
    sem_p, far_ready, sem_q, sem_k, sem_v, sem_t, sem_r, send_q, send_k, send_v, send_t, send_r,
):
    me = lax.axis_index("rows")
    local = q_in.shape[0]
    blocks = n // KV_HEADS
    block_rows = KV_HEADS * local
    my_block = me // KV_HEADS
    my_slot = me % KV_HEADS

    def send(src, dst, send_sem, recv_sem, to):
        pltpu.make_async_remote_copy(
            src_ref=src, dst_ref=dst, send_sem=send_sem, recv_sem=recv_sem,
            device_id={"rows": to}, device_id_type=MESH,
        ).start()

    def settle(ref, sem):
        pltpu.make_async_copy(ref, ref, sem).wait()

    def columns(ref, head, width):
        return ref.at[:, pl.ds(pl.multiple_of(head * width, width), width)]

    barrier = pltpu.get_barrier_semaphore()

    def greet(sem, to):
        pl.semaphore_signal(sem, inc=1, device_id={"rows": to}, device_id_type=MESH)

    others = [(my_block + far) % blocks for far in range(1, blocks)]
    heads = [(my_slot + step) % KV_HEADS for step in range(KV_HEADS)]
    for block in others:
        greet(barrier, block * KV_HEADS + my_slot)
    for head in heads[1:]:
        greet(barrier, my_block * KV_HEADS + head)
    pltpu.make_async_copy(columns(q_in, my_slot, WIDTH), qbuf.at[me], sem_q.at[my_block]).start()
    pltpu.make_async_copy(columns(pk_in, my_slot, HEAD_DIM), kbuf.at[my_slot], sem_k).start()
    pltpu.make_async_copy(columns(tk_in, my_slot, HEAD_DIM), tbuf.at[0, my_slot], sem_t.at[0]).start()
    pltpu.make_async_copy(columns(tv_in, my_slot, HEAD_DIM), tbuf.at[1, my_slot], sem_t.at[1]).start()
    pltpu.make_async_copy(columns(pv_in, my_slot, HEAD_DIM), vbuf.at[my_slot], sem_v).start()
    pltpu.make_async_copy(parents_in, parents, sem_p).start()
    pl.semaphore_wait(barrier, KV_HEADS - 1 + blocks - 1)

    for block in others:
        greet(far_ready, block * KV_HEADS + my_slot)
    for head in heads[1:]:
        to = my_block * KV_HEADS + head
        send(columns(tk_in, head, HEAD_DIM), tbuf.at[0, my_slot], send_t, sem_t.at[0], to)
        send(columns(pk_in, head, HEAD_DIM), kbuf.at[my_slot], send_k, sem_k, to)
        send(columns(q_in, head, WIDTH), qbuf.at[me], send_q, sem_q.at[my_block], to)
    if blocks > 1:
        pl.semaphore_wait(far_ready, blocks - 1)
    for block in others:
        for head in heads:
            to = block * KV_HEADS + head
            send(columns(q_in, head, WIDTH), qbuf.at[me], send_q, sem_q.at[my_block], to)
    for head in heads[1:]:
        to = my_block * KV_HEADS + head
        send(columns(tv_in, head, HEAD_DIM), tbuf.at[1, my_slot], send_t, sem_t.at[1], to)
        send(columns(pv_in, head, HEAD_DIM), vbuf.at[my_slot], send_v, sem_v, to)

    settle(parents, sem_p)
    count = parents.shape[1]
    parent = jnp.broadcast_to(parents[...], (count, count))
    token = lax.broadcasted_iota(jnp.int32, (count, count), 0)
    row = lax.broadcasted_iota(jnp.int32, (count, count), 1)
    hop = (parent == token).astype(jnp.float32).astype(jnp.bfloat16)
    mine = lax.broadcasted_iota(jnp.int32, (block_rows, count), 0) + my_block * block_rows
    own = lax.broadcasted_iota(jnp.int32, (block_rows, count), 1)
    member = (mine == own).astype(jnp.float32)
    seen = member
    for _ in range(TREE_DEPTH - 1):
        member = jnp.dot(member.astype(jnp.bfloat16), hop, preferred_element_type=jnp.float32)
        seen = seen + member
    same = (token == row).astype(jnp.float32).astype(jnp.bfloat16)
    mask[...] = lax.dot_general(
        same, seen.astype(jnp.bfloat16), LAST, preferred_element_type=jnp.float32
    )

    settle(kbuf, sem_k)
    keys = kbuf[...].reshape(-1, HEAD_DIM)
    settle(tbuf.at[0], sem_t.at[0])
    tree_keys = tbuf[0].astype(jnp.float32).reshape(block_rows, HEAD_DIM).astype(jnp.bfloat16)
    scale = HEAD_DIM ** (-0.5)

    def weigh(block):
        first = pl.multiple_of(block * KV_HEADS, KV_HEADS)
        settle(qbuf.at[pl.ds(0, KV_HEADS)], sem_q.at[block])
        queries = qbuf[pl.ds(first, KV_HEADS)].astype(jnp.float32).reshape(block_rows, WIDTH)
        visible = mask[pl.ds(pl.multiple_of(block * block_rows, block_rows), block_rows), :] > 0.5
        weights, maxima, masses = [], [], []
        for group in range(GROUPS):
            query = queries[:, group * HEAD_DIM : (group + 1) * HEAD_DIM].astype(jnp.bfloat16)
            slab = lax.dot_general(query, keys, LAST, preferred_element_type=jnp.float32) * scale
            tree = (
                lax.dot_general(query, tree_keys, LAST, preferred_element_type=jnp.float32) * scale
            )
            tree = jnp.where(visible, tree, -jnp.inf)
            top = jnp.maximum(
                jnp.max(slab, axis=1, keepdims=True), jnp.max(tree, axis=1, keepdims=True)
            )
            slab = jnp.exp(slab - top)
            tree = jnp.exp(tree - top)
            maxima.append(top)
            masses.append(
                jnp.sum(slab, axis=1, keepdims=True) + jnp.sum(tree, axis=1, keepdims=True)
            )
            weights.append((slab.astype(jnp.bfloat16), tree.astype(jnp.bfloat16)))
        stats = pack_stats(maxima, masses).reshape(KV_HEADS, local, HEAD_DIM)
        obuf[pl.ds(first, KV_HEADS), :, WIDTH:] = stats.astype(jnp.bfloat16)
        return weights

    def values_ready():
        settle(vbuf, sem_v)
        settle(tbuf.at[1], sem_t.at[1])

    def apply(block, weights, last):
        first = pl.multiple_of(block * KV_HEADS, KV_HEADS)
        values = vbuf[...].reshape(-1, HEAD_DIM)
        tree_values = tbuf[1].astype(jnp.float32).reshape(block_rows, HEAD_DIM).astype(jnp.bfloat16)
        for group, (slab, tree) in enumerate(weights):
            piece = jnp.dot(slab, values, preferred_element_type=jnp.float32) + jnp.dot(
                tree, tree_values, preferred_element_type=jnp.float32
            )
            piece = piece.reshape(KV_HEADS, local, HEAD_DIM).astype(jnp.bfloat16)
            obuf[pl.ds(first, KV_HEADS), :, group * HEAD_DIM : (group + 1) * HEAD_DIM] = piece
        for step in range(KV_HEADS):
            if last and step == 0:
                pltpu.make_async_copy(obuf.at[me], rbuf.at[me], sem_r).start()
            else:
                to = first + (my_slot + step) % KV_HEADS
                send(obuf.at[to], rbuf.at[me], send_r, sem_r, to)

    order = [(my_block + 1 + step) % blocks for step in range(blocks)]
    ahead = [weigh(block) for block in order[:2]]
    values_ready()
    for step, block in enumerate(order):
        weights = ahead[step] if step < 2 else weigh(block)
        apply(block, weights, step == blocks - 1)

    settle(qbuf.at[pl.ds(0, n - 1)], send_q)
    settle(kbuf.at[pl.ds(0, KV_HEADS - 1)], send_k)
    settle(vbuf.at[pl.ds(0, KV_HEADS - 1)], send_v)
    settle(tbuf.at[:, pl.ds(0, KV_HEADS - 1)], send_t)
    settle(rbuf, sem_r)

    stat = rbuf[:, :, WIDTH:].astype(jnp.float32).reshape(n * local, HEAD_DIM)
    stat = (
        stat
        + pltpu.roll(stat, HEAD_DIM - PART, 1)
        + pltpu.roll(stat, HEAD_DIM - 2 * PART, 1)
    ).reshape(blocks, block_rows, HEAD_DIM)
    top = jnp.max(stat, axis=0)
    lane = lax.broadcasted_iota(jnp.int32, (block_rows, HEAD_DIM), 1)
    factors = []
    total = jnp.zeros((block_rows, HEAD_DIM), jnp.float32)
    for block in range(blocks):
        factor = jnp.exp(stat[block] - top)
        mass = pltpu.roll(stat[block], HEAD_DIM - GROUPS, 1)
        total = total + factor * mass
        factors.append(factor)
    total = jnp.where(lane < GROUPS, total, 1.0)
    factors = [factor / total for factor in factors]
    for head in range(KV_HEADS):
        for group in range(GROUPS):
            result = jnp.zeros((local, HEAD_DIM), jnp.float32)
            for block in range(blocks):
                share = factors[block][head * local : (head + 1) * local, group : group + 1]
                piece = rbuf[block * KV_HEADS + head, :, group * HEAD_DIM : (group + 1) * HEAD_DIM]
                result = result + piece.astype(jnp.float32) * share
            at = head * WIDTH + group * HEAD_DIM
            out[:, at : at + HEAD_DIM] = result.astype(out.dtype)
    settle(rbuf.at[pl.ds(0, n - 1)], send_r)


def shards(n, queries, prefix_keys, prefix_values, tree_keys, tree_values, parents):
    local = queries.shape[0]
    tokens = prefix_keys.shape[0]
    kind = queries.dtype
    blocks = n // KV_HEADS
    hbm = pl.BlockSpec(memory_space=pl.ANY)
    vmem = pl.BlockSpec(memory_space=pltpu.VMEM)
    dma = pltpu.SemaphoreType.DMA
    return pl.pallas_call(
        functools.partial(kernel, n),
        out_shape=pltpu.VMEM(queries.shape, kind),
        in_specs=[hbm] * 6,
        out_specs=vmem,
        scratch_shapes=[
            pltpu.VMEM((n, local, WIDTH), kind),
            pltpu.VMEM((KV_HEADS, tokens, HEAD_DIM), kind),
            pltpu.VMEM((KV_HEADS, tokens, HEAD_DIM), kind),
            pltpu.VMEM((2, KV_HEADS, local, HEAD_DIM), kind),
            pltpu.VMEM((n, local, WIDTH + HEAD_DIM), kind),
            pltpu.VMEM((n, local, WIDTH + HEAD_DIM), kind),
            pltpu.VMEM((n * local, KV_HEADS * local), jnp.float32),
            pltpu.VMEM((1, n * local), jnp.int32),
            dma, pltpu.SemaphoreType.REGULAR, dma((blocks,)), dma, dma, dma((2,)), dma, dma, dma, dma, dma, dma,
        ],
        compiler_params=pltpu.CompilerParams(collective_id=0, has_side_effects=True),
        name="tree_attention",
    )(queries, prefix_keys, prefix_values, tree_keys, tree_values, parents.reshape(1, -1))


def solution(mesh):
    placed = (
        P(("group", "rows"), None),
        P(("group", "rows"), None),
        P(("group", "rows"), None),
        P(("group", "rows"), None),
        P(("group", "rows"), None),
        P("group"),
    )
    return jax.shard_map(
        functools.partial(shards, mesh.shape["rows"]),
        mesh=mesh,
        in_specs=placed,
        out_specs=P(("group", "rows"), None),
        check_vma=False,
    )
```

```python
import functools

import jax
import jax.numpy as jnp
from jax import lax
from jax.experimental import pallas as pl
from jax.experimental.pallas import tpu as pltpu
from jax.sharding import PartitionSpec as P

QUERY_HEADS = 24
KV_HEADS = 8
HEAD_DIM = 128
TREE_DEPTH = 4
GROUPS = QUERY_HEADS // KV_HEADS
WIDTH = GROUPS * HEAD_DIM
PART = 32

LAST = (((1,), (1,)), ((), ()))
MESH = pl.DeviceIdType.MESH


def pack_stats(maxima, masses):
    rows = maxima[0].shape[0]
    lane = lax.broadcasted_iota(jnp.int32, (rows, HEAD_DIM), 1)
    place = lane % PART
    stat = jnp.zeros((rows, HEAD_DIM), jnp.float32)
    for at, column in enumerate(maxima + masses):
        stat = jnp.where(place == at, column, stat)
    high = stat.astype(jnp.bfloat16).astype(jnp.float32)
    rest = stat - high
    middle = rest.astype(jnp.bfloat16).astype(jnp.float32)
    low = rest - middle
    return jnp.where(lane < PART, high, jnp.where(lane < 2 * PART, middle, low))


def kernel(
    n, q_in, pk_in, pv_in, tk_in, tv_in, parents_in, out,
    qbuf, kbuf, vbuf, tbuf, obuf, rbuf, mask, parents,
    q_at, pk_at, pv_at, tk_at, tv_at,
    sem_p, sem_s, far_ready, sem_q, sem_k, sem_v, sem_t, sem_r, send_q, send_k, send_v, send_t, send_r,
):
    me = lax.axis_index("rows")
    local = q_in.shape[0]
    blocks = n // KV_HEADS
    block_rows = KV_HEADS * local
    my_block = me // KV_HEADS
    my_slot = me % KV_HEADS

    def send(src, dst, send_sem, recv_sem, to):
        pltpu.make_async_remote_copy(
            src_ref=src, dst_ref=dst, send_sem=send_sem, recv_sem=recv_sem,
            device_id={"rows": to}, device_id_type=MESH,
        ).start()

    def settle(ref, sem):
        pltpu.make_async_copy(ref, ref, sem).wait()

    def columns(ref, head, width):
        return ref.at[:, pl.ds(pl.multiple_of(head * width, width), width)]

    barrier = pltpu.get_barrier_semaphore()

    def greet(sem, to):
        pl.semaphore_signal(sem, inc=1, device_id={"rows": to}, device_id_type=MESH)

    others = [(my_block + far) % blocks for far in range(1, blocks)]
    heads = [(my_slot + step) % KV_HEADS for step in range(KV_HEADS)]
    for block in others:
        greet(barrier, block * KV_HEADS + my_slot)
    for head in heads[1:]:
        greet(barrier, my_block * KV_HEADS + head)
    staged = ((pk_in, pk_at), (tk_in, tk_at), (q_in, q_at), (tv_in, tv_at), (pv_in, pv_at))
    staging = [
        pltpu.make_async_copy(here, there, sem_s.at[at])
        for at, (here, there) in enumerate(staged)
    ]
    for copy in staging:
        copy.start()
    pltpu.make_async_copy(columns(q_in, my_slot, WIDTH), qbuf.at[me], sem_q.at[my_block]).start()
    pltpu.make_async_copy(columns(pk_in, my_slot, HEAD_DIM), kbuf.at[my_slot], sem_k).start()
    pltpu.make_async_copy(columns(tk_in, my_slot, HEAD_DIM), tbuf.at[0, my_slot], sem_t.at[0]).start()
    pltpu.make_async_copy(columns(tv_in, my_slot, HEAD_DIM), tbuf.at[1, my_slot], sem_t.at[1]).start()
    pltpu.make_async_copy(columns(pv_in, my_slot, HEAD_DIM), vbuf.at[my_slot], sem_v).start()
    pltpu.make_async_copy(parents_in, parents, sem_p).start()
    for copy in staging:
        copy.wait()
    pl.semaphore_wait(barrier, KV_HEADS - 1 + blocks - 1)

    for block in others:
        greet(far_ready, block * KV_HEADS + my_slot)
    for head in heads[1:]:
        to = my_block * KV_HEADS + head
        send(columns(tk_at, head, HEAD_DIM), tbuf.at[0, my_slot], send_t, sem_t.at[0], to)
        send(columns(pk_at, head, HEAD_DIM), kbuf.at[my_slot], send_k, sem_k, to)
        send(columns(q_at, head, WIDTH), qbuf.at[me], send_q, sem_q.at[my_block], to)
    if blocks > 1:
        pl.semaphore_wait(far_ready, blocks - 1)
    for block in others:
        for head in heads:
            to = block * KV_HEADS + head
            send(columns(q_at, head, WIDTH), qbuf.at[me], send_q, sem_q.at[my_block], to)
    for head in heads[1:]:
        to = my_block * KV_HEADS + head
        send(columns(tv_at, head, HEAD_DIM), tbuf.at[1, my_slot], send_t, sem_t.at[1], to)
        send(columns(pv_at, head, HEAD_DIM), vbuf.at[my_slot], send_v, sem_v, to)

    settle(parents, sem_p)
    count = parents.shape[1]
    parent = jnp.broadcast_to(parents[...], (count, count))
    token = lax.broadcasted_iota(jnp.int32, (count, count), 0)
    row = lax.broadcasted_iota(jnp.int32, (count, count), 1)
    hop = (parent == token).astype(jnp.float32).astype(jnp.bfloat16)
    mine = lax.broadcasted_iota(jnp.int32, (block_rows, count), 0) + my_block * block_rows
    own = lax.broadcasted_iota(jnp.int32, (block_rows, count), 1)
    member = (mine == own).astype(jnp.float32)
    seen = member
    for _ in range(TREE_DEPTH - 1):
        member = jnp.dot(member.astype(jnp.bfloat16), hop, preferred_element_type=jnp.float32)
        seen = seen + member
    same = (token == row).astype(jnp.float32).astype(jnp.bfloat16)
    mask[...] = lax.dot_general(
        same, seen.astype(jnp.bfloat16), LAST, preferred_element_type=jnp.float32
    )

    settle(kbuf, sem_k)
    keys = kbuf[...].reshape(-1, HEAD_DIM)
    settle(tbuf.at[0], sem_t.at[0])
    tree_keys = tbuf[0].astype(jnp.float32).reshape(block_rows, HEAD_DIM).astype(jnp.bfloat16)
    scale = HEAD_DIM ** (-0.5)

    def weigh(block):
        first = pl.multiple_of(block * KV_HEADS, KV_HEADS)
        settle(qbuf.at[pl.ds(0, KV_HEADS)], sem_q.at[block])
        queries = qbuf[pl.ds(first, KV_HEADS)].astype(jnp.float32).reshape(block_rows, WIDTH)
        visible = mask[pl.ds(pl.multiple_of(block * block_rows, block_rows), block_rows), :] > 0.5
        weights, maxima, masses = [], [], []
        for group in range(GROUPS):
            query = queries[:, group * HEAD_DIM : (group + 1) * HEAD_DIM].astype(jnp.bfloat16)
            slab = lax.dot_general(query, keys, LAST, preferred_element_type=jnp.float32) * scale
            tree = (
                lax.dot_general(query, tree_keys, LAST, preferred_element_type=jnp.float32) * scale
            )
            tree = jnp.where(visible, tree, -jnp.inf)
            top = jnp.maximum(
                jnp.max(slab, axis=1, keepdims=True), jnp.max(tree, axis=1, keepdims=True)
            )
            slab = jnp.exp(slab - top)
            tree = jnp.exp(tree - top)
            maxima.append(top)
            masses.append(
                jnp.sum(slab, axis=1, keepdims=True) + jnp.sum(tree, axis=1, keepdims=True)
            )
            weights.append((slab.astype(jnp.bfloat16), tree.astype(jnp.bfloat16)))
        stats = pack_stats(maxima, masses).reshape(KV_HEADS, local, HEAD_DIM)
        obuf[pl.ds(first, KV_HEADS), :, WIDTH:] = stats.astype(jnp.bfloat16)
        return weights

    def values_ready():
        settle(vbuf, sem_v)
        settle(tbuf.at[1], sem_t.at[1])

    def apply(block, weights, last):
        first = pl.multiple_of(block * KV_HEADS, KV_HEADS)
        values = vbuf[...].reshape(-1, HEAD_DIM)
        tree_values = tbuf[1].astype(jnp.float32).reshape(block_rows, HEAD_DIM).astype(jnp.bfloat16)
        for group, (slab, tree) in enumerate(weights):
            piece = jnp.dot(slab, values, preferred_element_type=jnp.float32) + jnp.dot(
                tree, tree_values, preferred_element_type=jnp.float32
            )
            piece = piece.reshape(KV_HEADS, local, HEAD_DIM).astype(jnp.bfloat16)
            obuf[pl.ds(first, KV_HEADS), :, group * HEAD_DIM : (group + 1) * HEAD_DIM] = piece
        for step in range(KV_HEADS):
            if last and step == 0:
                pltpu.make_async_copy(obuf.at[me], rbuf.at[me], sem_r).start()
            else:
                to = first + (my_slot + step) % KV_HEADS
                send(obuf.at[to], rbuf.at[me], send_r, sem_r, to)

    order = [(my_block + 1 + step) % blocks for step in range(blocks)]
    ahead = [weigh(block) for block in order[:2]]
    values_ready()
    for step, block in enumerate(order):
        weights = ahead[step] if step < 2 else weigh(block)
        apply(block, weights, step == blocks - 1)

    settle(qbuf.at[pl.ds(0, n - 1)], send_q)
    settle(kbuf.at[pl.ds(0, KV_HEADS - 1)], send_k)
    settle(vbuf.at[pl.ds(0, KV_HEADS - 1)], send_v)
    settle(tbuf.at[:, pl.ds(0, KV_HEADS - 1)], send_t)
    settle(rbuf, sem_r)

    stat = rbuf[:, :, WIDTH:].astype(jnp.float32).reshape(n * local, HEAD_DIM)
    stat = (
        stat
        + pltpu.roll(stat, HEAD_DIM - PART, 1)
        + pltpu.roll(stat, HEAD_DIM - 2 * PART, 1)
    ).reshape(blocks, block_rows, HEAD_DIM)
    top = jnp.max(stat, axis=0)
    lane = lax.broadcasted_iota(jnp.int32, (block_rows, HEAD_DIM), 1)
    factors = []
    total = jnp.zeros((block_rows, HEAD_DIM), jnp.float32)
    for block in range(blocks):
        factor = jnp.exp(stat[block] - top)
        mass = pltpu.roll(stat[block], HEAD_DIM - GROUPS, 1)
        total = total + factor * mass
        factors.append(factor)
    total = jnp.where(lane < GROUPS, total, 1.0)
    factors = [factor / total for factor in factors]
    for head in range(KV_HEADS):
        for group in range(GROUPS):
            result = jnp.zeros((local, HEAD_DIM), jnp.float32)
            for block in range(blocks):
                share = factors[block][head * local : (head + 1) * local, group : group + 1]
                piece = rbuf[block * KV_HEADS + head, :, group * HEAD_DIM : (group + 1) * HEAD_DIM]
                result = result + piece.astype(jnp.float32) * share
            at = head * WIDTH + group * HEAD_DIM
            out[:, at : at + HEAD_DIM] = result.astype(out.dtype)
    settle(rbuf.at[pl.ds(0, n - 1)], send_r)


def shards(n, queries, prefix_keys, prefix_values, tree_keys, tree_values, parents):
    local = queries.shape[0]
    tokens = prefix_keys.shape[0]
    kind = queries.dtype
    blocks = n // KV_HEADS
    hbm = pl.BlockSpec(memory_space=pl.ANY)
    vmem = pl.BlockSpec(memory_space=pltpu.VMEM)
    dma = pltpu.SemaphoreType.DMA
    return pl.pallas_call(
        functools.partial(kernel, n),
        out_shape=pltpu.VMEM(queries.shape, kind),
        in_specs=[hbm] * 6,
        out_specs=vmem,
        scratch_shapes=[
            pltpu.VMEM((n, local, WIDTH), kind),
            pltpu.VMEM((KV_HEADS, tokens, HEAD_DIM), kind),
            pltpu.VMEM((KV_HEADS, tokens, HEAD_DIM), kind),
            pltpu.VMEM((2, KV_HEADS, local, HEAD_DIM), kind),
            pltpu.VMEM((n, local, WIDTH + HEAD_DIM), kind),
            pltpu.VMEM((n, local, WIDTH + HEAD_DIM), kind),
            pltpu.VMEM((n * local, KV_HEADS * local), jnp.float32),
            pltpu.VMEM((1, n * local), jnp.int32),
            pltpu.VMEM(queries.shape, kind), pltpu.VMEM(prefix_keys.shape, kind),
            pltpu.VMEM(prefix_keys.shape, kind), pltpu.VMEM(tree_keys.shape, kind),
            pltpu.VMEM(tree_keys.shape, kind),
            dma, dma((5,)), pltpu.SemaphoreType.REGULAR, dma((blocks,)), dma, dma, dma((2,)), dma, dma, dma, dma, dma, dma,
        ],
        compiler_params=pltpu.CompilerParams(collective_id=0, has_side_effects=True),
        name="tree_attention",
    )(queries, prefix_keys, prefix_values, tree_keys, tree_values, parents.reshape(1, -1))


def solution(mesh):
    placed = (
        P(("group", "rows"), None),
        P(("group", "rows"), None),
        P(("group", "rows"), None),
        P(("group", "rows"), None),
        P(("group", "rows"), None),
        P("group"),
    )
    return jax.shard_map(
        functools.partial(shards, mesh.shape["rows"]),
        mesh=mesh,
        in_specs=placed,
        out_specs=P(("group", "rows"), None),
        check_vma=False,
    )
```
